32 devices in a mesh: dp: 1, mp: 32 (over z, y, x, core).
Axes of the slice: x: 2, y: 2, z: 4, core: 2. Of those that a mesh axis runs over, the one named last changes fastest.
Arguments:
- activations: bfloat16 [2048, 8192], P('dp', 'mp'), may hold values from -6 to 6
- w_up: bfloat16 [5, 256, 32768], P(None, None, 'mp'), may hold values from -0.15625 to 0.15625
- w_down: bfloat16 [5, 32768, 256], P(None, 'mp'), may hold values from -0.078125 to 0.078125
- u_up: bfloat16 [8192, 128], P('mp'), may hold values from -0.0625 to 0.0625
- v_up: bfloat16 [128, 32768], P(None, 'mp'), may hold values from -0.5 to 0.5
- u_down: bfloat16 [32768, 128], P('mp'), may hold values from -0.03125 to 0.03125
- v_down: bfloat16 [128, 8192], P(None, 'mp'), may hold values from -0.5 to 0.5
- mask_up: int32 [4, 32], P(None, 'mp'), may hold values 0 or 1
- mask_down: int32 [4, 32], P(None, 'mp'), may hold values 0 or 1
- grad_y: bfloat16 [2048, 8192], P('dp', 'mp'), may hold values from -6 to 6
Outputs:
- output: bfloat16 [2048, 8192], P('dp', 'mp')
- grad_x: bfloat16 [2048, 8192], P('dp', 'mp')
- grad_w_up: float32 [5, 256, 32768], P(None, None, 'mp')
- grad_w_down: float32 [5, 32768, 256], P(None, 'mp')
- grad_u_up: float32 [8192, 128], P('mp')
- grad_v_up: float32 [128, 32768], P(None, 'mp')
- grad_u_down: float32 [32768, 128], P('mp')
- grad_v_down: float32 [128, 8192], P(None, 'mp')
The draws below stay inside these ranges and needn't reach their ends.
All inputs are finite; a program needn't handle non-finite values. No bound on the sum of `mask_up` or of `mask_down` on one device may be relied on, other than what follows from the above.
Results may differ from the reference program's by a relative error of at most 0.008.
Values may be sent and summed in bfloat16 or wider, within the bound.
A program may use at most 192 MiB of HBM per device.

```python
import jax
import jax.numpy as jnp

D = 8192
FF = 32768
RANK = 128
LEVELS = 4
TOKENS = 2048
DG = 256
HG = 1024
N_MP = 32


def touch_ends(drawn, stream_key, low, largest):
    index_at = [jax.random.randint(jax.random.fold_in(stream_key, axis), (), 0, length) for axis, length in enumerate(drawn.shape)]
    main_axis = drawn.shape.index(max(drawn.shape))
    next_to = index_at[:main_axis] + [(index_at[main_axis] + 1) % drawn.shape[main_axis]] + index_at[main_axis + 1:]
    return drawn.at[tuple(index_at)].set(low).at[tuple(next_to)].set(largest)


def level_of(stream_key, dims, pieces, low, top_value):
    def one(axis_at, shards_of):
        heights = jax.random.uniform(jax.random.fold_in(jax.random.fold_in(stream_key, 6), axis_at), (shards_of,), jnp.float32, low / len(pieces), top_value / len(pieces))
        return jnp.repeat(jnp.exp(heights), dims[axis_at] // shards_of).reshape((-1,) + (1,) * (len(dims) - axis_at - 1))

    gain = one(*pieces[0])
    for cut in pieces[1:]:
        gain = gain * one(*cut)
    return gain


def gaussian(rng, shape, deviation, limit, shards=(), held_as=jnp.bfloat16):
    drawn = jax.random.normal(rng, shape, jnp.float32) * deviation
    if len(shards) > 0:
        drawn = level_of(rng, shape, shards, -0.22, 0.18) * drawn
    return jnp.clip(drawn, min=-limit, max=limit).astype(held_as)


def setup_inputs(seed: int = 0) -> dict:
    splits = jax.random.split(jax.random.key(seed), 11)
    activations = gaussian(splits[0], (TOKENS, D), 1.0, 6.0, ((1, 32),))
    w_up = gaussian(splits[1], (LEVELS + 1, DG, FF), ((LEVELS + 1) * DG) ** -0.5, 0.15625, ((2, 32),))
    w_down = gaussian(splits[2], (LEVELS + 1, FF, DG), ((LEVELS + 1) * HG) ** -0.5, 0.078125, ((1, 32),))
    u_up = gaussian(splits[3], (D, RANK), D ** -0.5, 0.0625, ((0, 32),))
    v_up = gaussian(splits[4], (RANK, FF), RANK ** -0.5, 0.5, ((1, 32),))
    u_down = gaussian(splits[5], (FF, RANK), FF ** -0.5, 0.03125, ((0, 32),))
    v_down = gaussian(splits[6], (RANK, D), RANK ** -0.5, 0.5, ((1, 32),))
    mask_up = touch_ends((jax.random.randint(splits[7], (LEVELS, N_MP), 0, 4) < 3).astype(jnp.int32), jax.random.fold_in(splits[7], 1), 0, 1)
    mask_down = touch_ends((jax.random.randint(splits[8], (LEVELS, N_MP), 0, 4) < 3).astype(jnp.int32), jax.random.fold_in(splits[8], 1), 0, 1)
    grad_y = gaussian(splits[9], (TOKENS, D), 1.0, 6.0, ((1, 32),))
    return {"activations": activations, "w_up": w_up, "w_down": w_down, "u_up": u_up, "v_up": v_up, "u_down": u_down, "v_down": v_down, "mask_up": mask_up, "mask_down": mask_down, "grad_y": grad_y}


def gelu_tanh(value):
    return jax.nn.gelu(value, approximate=True)

def reference(activations, w_up, w_down, u_up, v_up, u_down, v_down, mask_up, mask_down, grad_y):
    f32 = jnp.float32
    groups = jnp.arange(N_MP, dtype=jnp.int32)
    x_blocks = activations.astype(f32).reshape(TOKENS, N_MP, DG)
    wu_blocks = w_up.astype(f32).reshape(LEVELS + 1, DG, N_MP, HG)
    wd_blocks = w_down.astype(f32).reshape(LEVELS + 1, N_MP, HG, DG)
    mu_float = mask_up.astype(f32)
    md_float = mask_down.astype(f32)
    z_up = jnp.dot(activations, u_up, preferred_element_type=f32).astype(jnp.bfloat16)
    pre = jnp.einsum('tgd,dgh->tgh', x_blocks, wu_blocks[0])
    for level in range(LEVELS):
        partner = jnp.bitwise_xor(groups, jnp.int32(1 << level))
        term = jnp.einsum('tgd,dgh->tgh', x_blocks[:, partner], wu_blocks[level + 1])
        pre = pre + term * mu_float[level][None, :, None]
    pre = pre.reshape(TOKENS, FF) + jnp.dot(z_up, v_up, preferred_element_type=f32)
    hidden = gelu_tanh(pre).astype(jnp.bfloat16)
    hid_blocks = hidden.astype(f32).reshape(TOKENS, N_MP, HG)
    z_down = jnp.dot(hidden, u_down, preferred_element_type=f32).astype(jnp.bfloat16)
    out = jnp.einsum('tgh,ghd->tgd', hid_blocks, wd_blocks[0])
    for level in range(LEVELS):
        partner = jnp.bitwise_xor(groups, jnp.int32(1 << level))
        term = jnp.einsum('tgh,ghd->tgd', hid_blocks[:, partner], wd_blocks[level + 1][partner])
        out = out + term * md_float[level][None, :, None]
    output = (out.reshape(TOKENS, D) + jnp.dot(z_down, v_down, preferred_element_type=f32)).astype(jnp.bfloat16)
    gy_blocks = grad_y.astype(f32).reshape(TOKENS, N_MP, DG)
    grad_v_down = jnp.dot(z_down.T, grad_y, preferred_element_type=f32)
    gz_down = jnp.dot(grad_y, v_down.T, preferred_element_type=f32).astype(jnp.bfloat16)
    grad_u_down = jnp.dot(hidden.T, gz_down, preferred_element_type=f32)
    gwd_list = [jnp.einsum('tgh,tgd->ghd', hid_blocks, gy_blocks)]
    grad_hid = jnp.einsum('tgd,ghd->tgh', gy_blocks, wd_blocks[0])
    for level in range(LEVELS):
        partner = jnp.bitwise_xor(groups, jnp.int32(1 << level))
        masked = gy_blocks[:, partner] * md_float[level][partner][None, :, None]
        gwd_list.append(jnp.einsum('tgh,tgd->ghd', hid_blocks, masked))
        grad_hid = grad_hid + jnp.einsum('tgd,ghd->tgh', masked, wd_blocks[level + 1])
    grad_w_down = jnp.stack(gwd_list).reshape(LEVELS + 1, FF, DG)
    grad_hid = grad_hid.reshape(TOKENS, FF) + jnp.dot(gz_down, u_down.T, preferred_element_type=f32)
    unused, pullback = jax.vjp(gelu_tanh, pre)
    grad_pre = pullback(grad_hid)[0].astype(jnp.bfloat16)
    grad_v_up = jnp.dot(z_up.T, grad_pre, preferred_element_type=f32)
    gz_up = jnp.dot(grad_pre, v_up.T, preferred_element_type=f32).astype(jnp.bfloat16)
    grad_u_up = jnp.dot(activations.T, gz_up, preferred_element_type=f32)
    gp_blocks = grad_pre.astype(f32).reshape(TOKENS, N_MP, HG)
    gwu_list = [jnp.einsum('tgd,tgh->dgh', x_blocks, gp_blocks)]
    grad_in = jnp.einsum('tgh,dgh->tgd', gp_blocks, wu_blocks[0])
    for level in range(LEVELS):
        partner = jnp.bitwise_xor(groups, jnp.int32(1 << level))
        gwu_list.append(jnp.einsum('tgd,tgh->dgh', x_blocks[:, partner], gp_blocks) * mu_float[level][None, :, None])
        masked = gp_blocks * mu_float[level][None, :, None]
        term = jnp.einsum('tgh,dgh->tgd', masked, wu_blocks[level + 1])
        grad_in = grad_in + term[:, partner]
    grad_w_up = jnp.stack(gwu_list).reshape(LEVELS + 1, DG, FF)
    grad_x = (grad_in.reshape(TOKENS, D) + jnp.dot(gz_up, u_up.T, preferred_element_type=f32)).astype(jnp.bfloat16)
    return (output, grad_x, grad_w_up, grad_w_down, grad_u_up, grad_v_up, grad_u_down, grad_v_down)
```

```python
import functools

import jax
import jax.numpy as jnp
from jax import lax
from jax.experimental import pallas as pl
from jax.experimental.pallas import tpu as pltpu
from jax.sharding import PartitionSpec as P

CHUNKS = 2
ROWS = 256
COLUMNS = 256
ROOT = 0.7978845608028654
CUBIC = 0.044715
VMEM_LIMIT = 56 * 1024 * 1024


def swapped(array, axis, distance):
    return lax.ppermute(array, axis, [(i, i ^ 1 << distance) for i in range(lax.axis_size(axis))])


def dot(left, right):
    return jnp.dot(left, right, preferred_element_type=jnp.float32)


def dot_nt(left, right):
    return lax.dot_general(left, right, (((1,), (1,)), ((), ())), preferred_element_type=jnp.float32)


def dot_tn(left, right):
    return lax.dot_general(left, right, (((0,), (0,)), ((), ())), preferred_element_type=jnp.float32)


def sums_kernel(slabs, mu_ref, md_ref, *refs):
    xs, gys = refs[:slabs], refs[slabs:2 * slabs]
    wu_ref, wd_ref, pre_ref, gh_ref = refs[2 * slabs:]
    left = [xs[0][...]]
    right = [gys[0][...]]
    for k in range(1, slabs):
        left.append(xs[k][...] * mu_ref[k - 1].astype(jnp.bfloat16))
        right.append(gys[k][...] * md_ref[k - 1].astype(jnp.bfloat16))
    hidden = wu_ref.shape[2]
    step = min(COLUMNS, hidden)
    for start in range(0, hidden, step):
        cols = slice(start, start + step)
        total = dot(left[0], wu_ref[0, :, cols])
        for k in range(1, slabs):
            total += dot(left[k], wu_ref[k, :, cols])
        pre_ref[:, cols] = total
        total = dot_nt(right[0], wd_ref[0, cols, :])
        for k in range(1, slabs):
            total += dot_nt(right[k], wd_ref[k, cols, :])
        gh_ref[:, cols] = total


def smem():
    return pl.BlockSpec(memory_space=pltpu.SMEM)


def fixed(array):
    zeros = (0,) * array.ndim
    return pl.BlockSpec(array.shape, lambda i: zeros, pipeline_mode=pl.Buffered(1))


def by_rows(width):
    return pl.BlockSpec((ROWS, width), lambda i: (i, 0))


def sums(mu, md_partner, xs, gys, w_up, w_down):
    slabs = len(xs)
    tokens, width = xs[0].shape
    hidden = w_up.shape[2]
    flops = 4 * slabs * tokens * width * hidden
    return pl.pallas_call(
        functools.partial(sums_kernel, slabs),
        grid=(tokens // ROWS,),
        in_specs=[smem(), smem()] + [by_rows(width)] * (2 * slabs) + [fixed(w_up), fixed(w_down)],
        out_specs=[by_rows(hidden)] * 2,
        out_shape=[jax.ShapeDtypeStruct((tokens, hidden), jnp.float32)] * 2,
        compiler_params=pltpu.CompilerParams(vmem_limit_bytes=VMEM_LIMIT),
        cost_estimate=pl.CostEstimate(flops=flops, bytes_accessed=8 * tokens * hidden + 4 * slabs * width * (tokens + hidden), transcendentals=0),
        name="sums",
    )(mu, md_partner, *xs, *gys, w_up, w_down)


def products_kernel(slabs, mu_ref, pre_ref, gh_ref, zs_ref, wu_ref, wd_ref, vu_ref, ud_ref, *outs):
    hid_ref, gp_ref, z_ref, out_ref, gx_ref = outs[:5]
    out_parts = outs[5:4 + slabs]
    gx_parts = outs[4 + slabs:3 + 2 * slabs]
    rank = vu_ref.shape[0]
    z_up = zs_ref[:, :rank]
    gz_down = zs_ref[:, rank:]
    hidden = wu_ref.shape[2]
    step = min(COLUMNS, hidden)
    for start in range(0, hidden, step):
        cols = slice(start, start + step)
        v = pre_ref[:, cols] + dot(z_up, vu_ref[:, cols])
        gh = gh_ref[:, cols] + dot_nt(gz_down, ud_ref[cols, :])
        square = v * v
        half_tanh = 0.5 * jnp.tanh(v * (ROOT + (ROOT * CUBIC) * square))
        gate = 0.5 + half_tanh
        hid_ref[:, cols] = (v * gate).astype(jnp.bfloat16)
        slope = gate + v * (0.5 - 2.0 * half_tanh * half_tanh) * (ROOT + (3.0 * ROOT * CUBIC) * square)
        gp_ref[:, cols] = (gh * slope).astype(jnp.bfloat16)
    hid = hid_ref[...]
    gp = gp_ref[...]
    for k in range(1, slabs):
        out_parts[k - 1][...] = dot(hid, wd_ref[k]).astype(jnp.bfloat16)
        gx_parts[k - 1][...] = (dot_nt(gp, wu_ref[k]) * mu_ref[k - 1]).astype(jnp.bfloat16)
    out_ref[...] = dot(hid, wd_ref[0])
    gx_ref[...] = dot_nt(gp, wu_ref[0])
    z_ref[:, :rank] = dot(hid, ud_ref[...])
    z_ref[:, rank:] = dot_nt(gp, vu_ref[...])


def products(mu, pre, gh, zs, w_up, w_down, v_up, u_down):
    slabs, width, hidden = w_up.shape
    tokens = pre.shape[0]
    rank = v_up.shape[0]
    levels = slabs - 1
    shape = lambda n, dtype: jax.ShapeDtypeStruct((tokens, n), dtype)
    flops = 4 * tokens * hidden * (slabs * width + 2 * rank)
    got = pl.pallas_call(
        functools.partial(products_kernel, slabs),
        grid=(tokens // ROWS,),
        in_specs=[smem(), by_rows(hidden), by_rows(hidden), by_rows(2 * rank), fixed(w_up), fixed(w_down), fixed(v_up), fixed(u_down)],
        out_specs=[by_rows(hidden)] * 2 + [by_rows(2 * rank)] + [by_rows(width)] * (2 + 2 * levels),
        out_shape=[shape(hidden, jnp.bfloat16)] * 2 + [shape(2 * rank, jnp.float32)] + [shape(width, jnp.float32)] * 2 + [shape(width, jnp.bfloat16)] * (2 * levels),
        compiler_params=pltpu.CompilerParams(vmem_limit_bytes=VMEM_LIMIT),
        cost_estimate=pl.CostEstimate(flops=flops, bytes_accessed=12 * tokens * hidden + 4 * slabs * width * (tokens + hidden), transcendentals=tokens * hidden),
        name="products",
    )(mu, pre, gh, zs, w_up, w_down, v_up, u_down)
    return got[0], got[1], got[2], got[3], got[4], got[5:5 + levels], got[5 + levels:]


def low_rank_sum(partial):
    mine = lax.psum_scatter(partial, "mp", scatter_dimension=0, tiled=True)
    return lax.all_gather(mine.astype(jnp.bfloat16), "mp", axis=0, tiled=True)


def summed_over_dp(array):
    if lax.axis_size("dp") == 1:
        return array
    return lax.psum(array.astype(jnp.bfloat16), "dp").astype(jnp.float32)


def per_device(activations, w_up, w_down, u_up, v_up, u_down, v_down, mask_up, mask_down, grad_y):
    levels = mask_up.shape[0]
    slabs = levels + 1
    rank = v_up.shape[0]
    tokens = activations.shape[0]
    size = tokens // CHUNKS
    mu = mask_up[:, 0].astype(jnp.float32)
    md = mask_down[:, 0].astype(jnp.float32)
    zs = low_rank_sum(jnp.concatenate([dot(activations, u_up), dot_nt(grad_y, v_down)], axis=1))
    md_partner = jnp.concatenate([swapped(md[k:k + 1], "mp", k) for k in range(levels)])
    x_chunks, gy_chunks = [], []
    for c in range(CHUNKS):
        x = activations[c * size:(c + 1) * size]
        gy = grad_y[c * size:(c + 1) * size]
        x_chunks.append([x] + [swapped(x, "mp", k) for k in range(levels)])
        gy_chunks.append([gy] + [swapped(gy, "mp", k) for k in range(levels)])
    stages = []
    for c in range(CHUNKS):
        pre, gh = sums(mu, md_partner, x_chunks[c], gy_chunks[c], w_up, w_down)
        stages.append(products(mu, pre, gh, zs[c * size:(c + 1) * size], w_up, w_down, v_up, u_down))
    outputs, grad_xs, z_lates = [], [], []
    for c in range(CHUNKS):
        hid, gp, z_part, out, gx, out_parts, gx_parts = stages[c]
        z_late = low_rank_sum(z_part)
        z_lates.append(z_late)
        out = out + dot(z_late[:, :rank], v_down)
        gx = gx + dot_nt(z_late[:, rank:], u_up)
        for k in range(levels):
            out = out + md[k] * swapped(out_parts[k], "mp", k).astype(jnp.float32)
            gx = gx + swapped(gx_parts[k], "mp", k).astype(jnp.float32)
        outputs.append(out.astype(jnp.bfloat16))
        grad_xs.append(gx.astype(jnp.bfloat16))
    z_late = jnp.concatenate(z_lates)
    grad_w_down, grad_w_up = [], []
    for k in range(slabs):
        down = sum(dot_tn(stages[c][0], gy_chunks[c][k]) for c in range(CHUNKS))
        up = sum(dot_tn(x_chunks[c][k], stages[c][1]) for c in range(CHUNKS))
        grad_w_down.append(down if k == 0 else down * md_partner[k - 1])
        grad_w_up.append(up if k == 0 else up * mu[k - 1])
    grads = (
        jnp.stack(grad_w_up),
        jnp.stack(grad_w_down),
        dot_tn(activations, z_late[:, rank:]),
        sum(dot_tn(zs[c * size:(c + 1) * size, :rank], stages[c][1]) for c in range(CHUNKS)),
        sum(dot_tn(stages[c][0], zs[c * size:(c + 1) * size, rank:]) for c in range(CHUNKS)),
        dot_tn(z_late[:, :rank], grad_y),
    )
    grads = tuple(summed_over_dp(g) for g in grads)
    return (jnp.concatenate(outputs), jnp.concatenate(grad_xs)) + grads


def solution(mesh):
    placed = (
        P("dp", "mp"),
        P(None, None, "mp"),
        P(None, "mp", None),
        P("mp", None),
        P(None, "mp"),
        P("mp", None),
        P(None, "mp"),
        P(None, "mp"),
        P(None, "mp"),
        P("dp", "mp"),
    )
    return jax.shard_map(
        per_device,
        mesh=mesh,
        in_specs=placed,
        out_specs=(
            P("dp", "mp"),
            P("dp", "mp"),
            P(None, None, "mp"),
            P(None, "mp", None),
            P("mp", None),
            P(None, "mp"),
            P("mp", None),
            P(None, "mp"),
        ),
        check_vma=False,
    )
```

```python
import functools

import jax
import jax.numpy as jnp
from jax import lax
from jax.experimental import pallas as pl
from jax.experimental.pallas import tpu as pltpu
from jax.sharding import PartitionSpec as P

CHUNKS = 2
ROWS = 256
COLUMNS = 256
ROOT = 0.7978845608028654
CUBIC = 0.044715
VMEM_LIMIT = 56 * 1024 * 1024


def swapped(array, axis, distance):
    return lax.ppermute(array, axis, [(i, i ^ 1 << distance) for i in range(lax.axis_size(axis))])


def dot(left, right):
    return jnp.dot(left, right, preferred_element_type=jnp.float32)


def dot_nt(left, right):
    return lax.dot_general(left, right, (((1,), (1,)), ((), ())), preferred_element_type=jnp.float32)


def dot_tn(left, right):
    return lax.dot_general(left, right, (((0,), (0,)), ((), ())), preferred_element_type=jnp.float32)


def sums_kernel(slabs, mu_ref, md_ref, *refs):
    x_ref, gy_ref = refs[:2]
    pairs = refs[2:1 + slabs]
    wu_ref, wd_ref, pre_ref, gh_ref = refs[1 + slabs:]
    width = x_ref.shape[1]
    left = [x_ref[...]]
    right = [gy_ref[...]]
    for k in range(slabs - 1):
        left.append(pairs[k][:, :width] * mu_ref[k].astype(jnp.bfloat16))
        right.append(pairs[k][:, width:] * md_ref[k].astype(jnp.bfloat16))
    hidden = wu_ref.shape[2]
    step = min(COLUMNS, hidden)
    for start in range(0, hidden, step):
        cols = slice(start, start + step)
        total = dot(left[0], wu_ref[0, :, cols])
        for k in range(1, slabs):
            total += dot(left[k], wu_ref[k, :, cols])
        pre_ref[:, cols] = total
        total = dot_nt(right[0], wd_ref[0, cols, :])
        for k in range(1, slabs):
            total += dot_nt(right[k], wd_ref[k, cols, :])
        gh_ref[:, cols] = total


def smem():
    return pl.BlockSpec(memory_space=pltpu.SMEM)


def fixed(array):
    zeros = (0,) * array.ndim
    return pl.BlockSpec(array.shape, lambda i: zeros, pipeline_mode=pl.Buffered(1))


def by_rows(width):
    return pl.BlockSpec((ROWS, width), lambda i: (i, 0))


def sums(mu, md_partner, x, gy, pairs, w_up, w_down):
    slabs = len(pairs) + 1
    tokens, width = x.shape
    hidden = w_up.shape[2]
    flops = 4 * slabs * tokens * width * hidden
    return pl.pallas_call(
        functools.partial(sums_kernel, slabs),
        grid=(tokens // ROWS,),
        in_specs=[smem(), smem()] + [by_rows(width)] * 2 + [by_rows(2 * width)] * (slabs - 1) + [fixed(w_up), fixed(w_down)],
        out_specs=[by_rows(hidden)] * 2,
        out_shape=[jax.ShapeDtypeStruct((tokens, hidden), jnp.float32)] * 2,
        compiler_params=pltpu.CompilerParams(vmem_limit_bytes=VMEM_LIMIT),
        cost_estimate=pl.CostEstimate(flops=flops, bytes_accessed=8 * tokens * hidden + 4 * slabs * width * (tokens + hidden), transcendentals=0),
        name="sums",
    )(mu, md_partner, x, gy, *pairs, w_up, w_down)


def products_kernel(slabs, mu_ref, pre_ref, gh_ref, zs_ref, wu_ref, wd_ref, vu_ref, ud_ref, *outs):
    hid_ref, gp_ref, z_ref, out_ref, gx_ref = outs[:5]
    parts = outs[5:4 + slabs]
    width = wu_ref.shape[1]
    rank = vu_ref.shape[0]
    z_up = zs_ref[:, :rank]
    gz_down = zs_ref[:, rank:]
    hidden = wu_ref.shape[2]
    step = min(COLUMNS, hidden)
    for start in range(0, hidden, step):
        cols = slice(start, start + step)
        v = pre_ref[:, cols] + dot(z_up, vu_ref[:, cols])
        gh = gh_ref[:, cols] + dot_nt(gz_down, ud_ref[cols, :])
        square = v * v
        half_tanh = 0.5 * jnp.tanh(v * (ROOT + (ROOT * CUBIC) * square))
        gate = 0.5 + half_tanh
        hid_ref[:, cols] = (v * gate).astype(jnp.bfloat16)
        slope = gate + v * (0.5 - 2.0 * half_tanh * half_tanh) * (ROOT + (3.0 * ROOT * CUBIC) * square)
        gp_ref[:, cols] = (gh * slope).astype(jnp.bfloat16)
    hid = hid_ref[...]
    gp = gp_ref[...]
    for k in range(1, slabs):
        parts[k - 1][:, :width] = dot(hid, wd_ref[k]).astype(jnp.bfloat16)
        parts[k - 1][:, width:] = (dot_nt(gp, wu_ref[k]) * mu_ref[k - 1]).astype(jnp.bfloat16)
    out_ref[...] = dot(hid, wd_ref[0])
    gx_ref[...] = dot_nt(gp, wu_ref[0])
    z_ref[:, :rank] = dot(hid, ud_ref[...])
    z_ref[:, rank:] = dot_nt(gp, vu_ref[...])


def products(mu, pre, gh, zs, w_up, w_down, v_up, u_down):
    slabs, width, hidden = w_up.shape
    tokens = pre.shape[0]
    rank = v_up.shape[0]
    levels = slabs - 1
    shape = lambda n, dtype: jax.ShapeDtypeStruct((tokens, n), dtype)
    flops = 4 * tokens * hidden * (slabs * width + 2 * rank)
    got = pl.pallas_call(
        functools.partial(products_kernel, slabs),
        grid=(tokens // ROWS,),
        in_specs=[smem(), by_rows(hidden), by_rows(hidden), by_rows(2 * rank), fixed(w_up), fixed(w_down), fixed(v_up), fixed(u_down)],
        out_specs=[by_rows(hidden)] * 2 + [by_rows(2 * rank)] + [by_rows(width)] * 2 + [by_rows(2 * width)] * levels,
        out_shape=[shape(hidden, jnp.bfloat16)] * 2 + [shape(2 * rank, jnp.float32)] + [shape(width, jnp.float32)] * 2 + [shape(2 * width, jnp.bfloat16)] * levels,
        compiler_params=pltpu.CompilerParams(vmem_limit_bytes=VMEM_LIMIT),
        cost_estimate=pl.CostEstimate(flops=flops, bytes_accessed=12 * tokens * hidden + 4 * slabs * width * (tokens + hidden), transcendentals=tokens * hidden),
        name="products",
    )(mu, pre, gh, zs, w_up, w_down, v_up, u_down)
    return got[0], got[1], got[2], got[3], got[4], got[5:]


def low_rank_sum(partial):
    rounds = lax.axis_size("mp").bit_length() - 1
    index = lax.axis_index("mp")
    held = partial
    for level in range(rounds):
        bit = (index >> level) & 1
        half = held.shape[0] // 2
        sent = lax.dynamic_slice_in_dim(held, (1 - bit) * half, half)
        kept = lax.dynamic_slice_in_dim(held, bit * half, half)
        held = kept + swapped(sent.astype(jnp.bfloat16), "mp", level).astype(jnp.float32)
    held = held.astype(jnp.bfloat16)
    for level in reversed(range(rounds)):
        bit = (index >> level) & 1
        other = swapped(held, "mp", level)
        held = jnp.concatenate([jnp.where(bit == 0, held, other), jnp.where(bit == 0, other, held)])
    return held


def summed_over_dp(array):
    if lax.axis_size("dp") == 1:
        return array
    return lax.psum(array.astype(jnp.bfloat16), "dp").astype(jnp.float32)


def per_device(activations, w_up, w_down, u_up, v_up, u_down, v_down, mask_up, mask_down, grad_y):
    levels = mask_up.shape[0]
    slabs = levels + 1
    rank = v_up.shape[0]
    tokens = activations.shape[0]
    size = tokens // CHUNKS
    mu = mask_up[:, 0].astype(jnp.float32)
    md = mask_down[:, 0].astype(jnp.float32)
    zs = low_rank_sum(jnp.concatenate([dot(activations, u_up), dot_nt(grad_y, v_down)], axis=1))
    md_partner = jnp.concatenate([swapped(md[k:k + 1], "mp", k) for k in range(levels)])
    width = activations.shape[1]
    both = jnp.concatenate([activations, grad_y], axis=1)
    pairs = []
    for c in range(CHUNKS):
        if c == 1:
            both, zs = lax.optimization_barrier((both, zs))
        pairs.append([swapped(both[c * size:(c + 1) * size], "mp", k) for k in range(levels)])
    x_chunks = [[activations[c * size:(c + 1) * size]] + [p[:, :width] for p in pairs[c]] for c in range(CHUNKS)]
    gy_chunks = [[grad_y[c * size:(c + 1) * size]] + [p[:, width:] for p in pairs[c]] for c in range(CHUNKS)]
    stages, arrived = [], []
    for c in range(CHUNKS):
        pre, gh = sums(mu, md_partner, x_chunks[c][0], gy_chunks[c][0], pairs[c], w_up, w_down)
        stages.append(products(mu, pre, gh, zs[c * size:(c + 1) * size], w_up, w_down, v_up, u_down))
        arrived.append([swapped(stages[c][5][k], "mp", k) for k in range(levels)])
    z_late = low_rank_sum(jnp.concatenate([stage[2] for stage in stages]))
    outputs, grad_xs = [], []
    for c in range(CHUNKS):
        rows = slice(c * size, (c + 1) * size)
        out = stages[c][3] + dot(z_late[rows, :rank], v_down)
        gx = stages[c][4] + dot_nt(z_late[rows, rank:], u_up)
        for k in range(levels):
            out = out + md[k] * arrived[c][k][:, :width].astype(jnp.float32)
            gx = gx + arrived[c][k][:, width:].astype(jnp.float32)
        outputs.append(out.astype(jnp.bfloat16))
        grad_xs.append(gx.astype(jnp.bfloat16))
    grad_w_down, grad_w_up = [], []
    for k in range(slabs):
        down = sum(dot_tn(stages[c][0], gy_chunks[c][k]) for c in range(CHUNKS))
        up = sum(dot_tn(x_chunks[c][k], stages[c][1]) for c in range(CHUNKS))
        grad_w_down.append(down if k == 0 else down * md_partner[k - 1])
        grad_w_up.append(up if k == 0 else up * mu[k - 1])
    grads = (
        jnp.stack(grad_w_up),
        jnp.stack(grad_w_down),
        dot_tn(activations, z_late[:, rank:]),
        sum(dot_tn(zs[c * size:(c + 1) * size, :rank], stages[c][1]) for c in range(CHUNKS)),
        sum(dot_tn(stages[c][0], zs[c * size:(c + 1) * size, rank:]) for c in range(CHUNKS)),
        dot_tn(z_late[:, :rank], grad_y),
    )
    grads = tuple(summed_over_dp(g) for g in grads)
    return (jnp.concatenate(outputs), jnp.concatenate(grad_xs)) + grads


def solution(mesh):
    placed = (
        P("dp", "mp"),
        P(None, None, "mp"),
        P(None, "mp", None),
        P("mp", None),
        P(None, "mp"),
        P("mp", None),
        P(None, "mp"),
        P(None, "mp"),
        P(None, "mp"),
        P("dp", "mp"),
    )
    return jax.shard_map(
        per_device,
        mesh=mesh,
        in_specs=placed,
        out_specs=(
            P("dp", "mp"),
            P("dp", "mp"),
            P(None, None, "mp"),
            P(None, "mp", None),
            P("mp", None),
            P(None, "mp"),
            P("mp", None),
            P(None, "mp"),
        ),
        check_vma=False,
    )
```

```python
import functools

import jax
import jax.numpy as jnp
from jax import lax
from jax.experimental import pallas as pl
from jax.experimental.pallas import tpu as pltpu
from jax.sharding import PartitionSpec as P


CHUNKS = 2
ROWS = 256
COLUMNS = 256
ROOT = 0.7978845608028654
CUBIC = 0.044715
VMEM_LIMIT = 56 * 1024 * 1024


def swapped(array, axis, distance):
    return lax.ppermute(array, axis, [(i, i ^ 1 << distance) for i in range(lax.axis_size(axis))])


def dot(left, right):
    return jnp.dot(left, right, preferred_element_type=jnp.float32)


def dot_nt(left, right):
    return lax.dot_general(left, right, (((1,), (1,)), ((), ())), preferred_element_type=jnp.float32)


def dot_tn(left, right):
    return lax.dot_general(left, right, (((0,), (0,)), ((), ())), preferred_element_type=jnp.float32)


def sums_kernel(slabs, mu_ref, md_ref, *refs):
    x_ref, gy_ref = refs[:2]
    pairs = refs[2:1 + slabs]
    wu_ref, wd_ref, pre_ref, gh_ref = refs[1 + slabs:]
    width = x_ref.shape[1]
    left = [x_ref[...]]
    right = [gy_ref[...]]
    for k in range(slabs - 1):
        left.append(pairs[k][:, :width] * mu_ref[k].astype(jnp.bfloat16))
        right.append(pairs[k][:, width:] * md_ref[k].astype(jnp.bfloat16))
    hidden = wu_ref.shape[2]
    step = min(COLUMNS, hidden)
    for start in range(0, hidden, step):
        cols = slice(start, start + step)
        total = dot(left[0], wu_ref[0, :, cols])
        for k in range(1, slabs):
            total += dot(left[k], wu_ref[k, :, cols])
        pre_ref[:, cols] = total
        total = dot_nt(right[0], wd_ref[0, cols, :])
        for k in range(1, slabs):
            total += dot_nt(right[k], wd_ref[k, cols, :])
        gh_ref[:, cols] = total


def smem():
    return pl.BlockSpec(memory_space=pltpu.SMEM)


def fixed(array):
    zeros = (0,) * array.ndim
    return pl.BlockSpec(array.shape, lambda i: zeros, pipeline_mode=pl.Buffered(1))


def by_rows(width):
    return pl.BlockSpec((ROWS, width), lambda i: (i, 0))


def sums(mu, md_partner, x, gy, pairs, w_up, w_down):
    slabs = len(pairs) + 1
    tokens, width = x.shape
    hidden = w_up.shape[2]
    flops = 4 * slabs * tokens * width * hidden
    return pl.pallas_call(
        functools.partial(sums_kernel, slabs),
        grid=(tokens // ROWS,),
        in_specs=[smem(), smem()] + [by_rows(width)] * 2 + [by_rows(2 * width)] * (slabs - 1) + [fixed(w_up), fixed(w_down)],
        out_specs=[by_rows(hidden)] * 2,
        out_shape=[jax.ShapeDtypeStruct((tokens, hidden), jnp.float32)] * 2,
        compiler_params=pltpu.CompilerParams(vmem_limit_bytes=VMEM_LIMIT),
        cost_estimate=pl.CostEstimate(flops=flops, bytes_accessed=8 * tokens * hidden + 4 * slabs * width * (tokens + hidden), transcendentals=0),
        name="sums",
    )(mu, md_partner, x, gy, *pairs, w_up, w_down)


def products_kernel(slabs, mu_ref, pre_ref, gh_ref, zs_ref, wu_ref, wd_ref, vu_ref, ud_ref, *outs):
    hid_ref, gp_ref, z_ref, out_ref, gx_ref = outs[:5]
    parts = outs[5:4 + slabs]
    width = wu_ref.shape[1]
    rank = vu_ref.shape[0]
    z_up = zs_ref[:, :rank]
    gz_down = zs_ref[:, rank:]
    hidden = wu_ref.shape[2]
    step = min(COLUMNS, hidden)
    for start in range(0, hidden, step):
        cols = slice(start, start + step)
        v = pre_ref[:, cols] + dot(z_up, vu_ref[:, cols])
        gh = gh_ref[:, cols] + dot_nt(gz_down, ud_ref[cols, :])
        square = v * v
        half_tanh = 0.5 * jnp.tanh(v * (ROOT + (ROOT * CUBIC) * square))
        gate = 0.5 + half_tanh
        hid_ref[:, cols] = (v * gate).astype(jnp.bfloat16)
        slope = gate + v * (0.5 - 2.0 * half_tanh * half_tanh) * (ROOT + (3.0 * ROOT * CUBIC) * square)
        gp_ref[:, cols] = (gh * slope).astype(jnp.bfloat16)
    hid = hid_ref[...]
    gp = gp_ref[...]
    for k in range(1, slabs):
        parts[k - 1][:, :width] = dot(hid, wd_ref[k]).astype(jnp.bfloat16)
        parts[k - 1][:, width:] = (dot_nt(gp, wu_ref[k]) * mu_ref[k - 1]).astype(jnp.bfloat16)
    out_ref[...] = dot(hid, wd_ref[0])
    gx_ref[...] = dot_nt(gp, wu_ref[0])
    z_ref[:, :rank] = dot(hid, ud_ref[...])
    z_ref[:, rank:] = dot_nt(gp, vu_ref[...])


def products(mu, pre, gh, zs, w_up, w_down, v_up, u_down):
    slabs, width, hidden = w_up.shape
    tokens = pre.shape[0]
    rank = v_up.shape[0]
    levels = slabs - 1
    shape = lambda n, dtype: jax.ShapeDtypeStruct((tokens, n), dtype)
    flops = 4 * tokens * hidden * (slabs * width + 2 * rank)
    got = pl.pallas_call(
        functools.partial(products_kernel, slabs),
        grid=(tokens // ROWS,),
        in_specs=[smem(), by_rows(hidden), by_rows(hidden), by_rows(2 * rank), fixed(w_up), fixed(w_down), fixed(v_up), fixed(u_down)],
        out_specs=[by_rows(hidden)] * 2 + [by_rows(2 * rank)] + [by_rows(width)] * 2 + [by_rows(2 * width)] * levels,
        out_shape=[shape(hidden, jnp.bfloat16)] * 2 + [shape(2 * rank, jnp.float32)] + [shape(width, jnp.float32)] * 2 + [shape(2 * width, jnp.bfloat16)] * levels,
        compiler_params=pltpu.CompilerParams(vmem_limit_bytes=VMEM_LIMIT),
        cost_estimate=pl.CostEstimate(flops=flops, bytes_accessed=12 * tokens * hidden + 4 * slabs * width * (tokens + hidden), transcendentals=tokens * hidden),
        name="products",
    )(mu, pre, gh, zs, w_up, w_down, v_up, u_down)
    return got[0], got[1], got[2], got[3], got[4], got[5:]


def low_rank_sum(partial):
    rounds = lax.axis_size("mp").bit_length() - 1
    index = lax.axis_index("mp")
    held = partial
    for level in range(rounds):
        bit = (index >> level) & 1
        half = held.shape[0] // 2
        sent = lax.dynamic_slice_in_dim(held, (1 - bit) * half, half)
        kept = lax.dynamic_slice_in_dim(held, bit * half, half)
        other = swapped(sent.astype(jnp.bfloat16) if level == 1 else sent, "mp", level)
        held = kept + other.astype(jnp.float32)
    held = held.astype(jnp.bfloat16)
    steps = {}
    for level in reversed(range(rounds)):
        bit = (index >> level) & 1
        other = swapped(held, "mp", level)
        steps[level] = other
        held = jnp.concatenate([jnp.where(bit == 0, held, other), jnp.where(bit == 0, other, held)])
    return held, steps


def summed_over_dp(array):
    if lax.axis_size("dp") == 1:
        return array
    return lax.psum(array.astype(jnp.bfloat16), "dp").astype(jnp.float32)


def sublayer(activations, w_up, w_down, u_up, v_up, u_down, v_down, mask_up, mask_down, grad_y):
    levels = mask_up.shape[0]
    slabs = levels + 1
    rank = v_up.shape[0]
    tokens = activations.shape[0]
    size = tokens // CHUNKS
    mu = mask_up[:, 0].astype(jnp.float32)
    md = mask_down[:, 0].astype(jnp.float32)
    zs, early = low_rank_sum(jnp.concatenate([dot(activations, u_up), dot_nt(grad_y, v_down)], axis=1))
    md_parts = []
    for k in range(levels):
        md_parts.append(swapped(md[k:k + 1], "mp", k))
    md_partner = jnp.concatenate(md_parts)
    width = activations.shape[1]
    pairs = []
    for c in range(CHUNKS):
        rows = slice(c * size, (c + 1) * size)
        both = jnp.concatenate([activations[rows], grad_y[rows]], axis=1)
        received = []
        for k in range(levels):
            sent = both if c == 0 else lax.optimization_barrier((both, early[k]))[0]
            received.append(swapped(sent, "mp", k))
        pairs.append(received)
    x_chunks = [[activations[c * size:(c + 1) * size]] + [p[:, :width] for p in pairs[c]] for c in range(CHUNKS)]
    gy_chunks = [[grad_y[c * size:(c + 1) * size]] + [p[:, width:] for p in pairs[c]] for c in range(CHUNKS)]
    stages, arrived = [], []
    for c in range(CHUNKS):
        pre, gh = sums(mu, md_partner, x_chunks[c][0], gy_chunks[c][0], pairs[c], w_up, w_down)
        stages.append(products(mu, pre, gh, zs[c * size:(c + 1) * size], w_up, w_down, v_up, u_down))
        received = []
        for k in range(levels):
            received.append(swapped(stages[c][5][k], "mp", k))
        arrived.append(received)
    z_late = low_rank_sum(jnp.concatenate([stage[2] for stage in stages]))[0]
    outputs, grad_xs = [], []
    for c in range(CHUNKS):
        rows = slice(c * size, (c + 1) * size)
        out = stages[c][3] + dot(z_late[rows, :rank], v_down)
        gx = stages[c][4] + dot_nt(z_late[rows, rank:], u_up)
        for k in range(levels):
            out = out + md[k] * arrived[c][k][:, :width].astype(jnp.float32)
            gx = gx + arrived[c][k][:, width:].astype(jnp.float32)
        outputs.append(out.astype(jnp.bfloat16))
        grad_xs.append(gx.astype(jnp.bfloat16))
    grad_w_down, grad_w_up = [], []
    for k in range(slabs):
        down = sum(dot_tn(stages[c][0], gy_chunks[c][k]) for c in range(CHUNKS))
        up = sum(dot_tn(x_chunks[c][k], stages[c][1]) for c in range(CHUNKS))
        grad_w_down.append(down if k == 0 else down * md_partner[k - 1])
        grad_w_up.append(up if k == 0 else up * mu[k - 1])
    grads = (
        jnp.stack(grad_w_up),
        jnp.stack(grad_w_down),
        dot_tn(activations, z_late[:, rank:]),
        sum(dot_tn(zs[c * size:(c + 1) * size, :rank], stages[c][1]) for c in range(CHUNKS)),
        sum(dot_tn(stages[c][0], zs[c * size:(c + 1) * size, rank:]) for c in range(CHUNKS)),
        dot_tn(z_late[:, :rank], grad_y),
    )
    grads = tuple(summed_over_dp(g) for g in grads)
    return (jnp.concatenate(outputs), jnp.concatenate(grad_xs)) + grads


def solution(mesh):
    placed = (
        P("dp", "mp"),
        P(None, None, "mp"),
        P(None, "mp", None),
        P("mp", None),
        P(None, "mp"),
        P("mp", None),
        P(None, "mp"),
        P(None, "mp"),
        P(None, "mp"),
        P("dp", "mp"),
    )
    return jax.shard_map(
        sublayer,
        mesh=mesh,
        in_specs=placed,
        out_specs=(
            P("dp", "mp"),
            P("dp", "mp"),
            P(None, None, "mp"),
            P(None, "mp", None),
            P("mp", None),
            P(None, "mp"),
            P("mp", None),
            P(None, "mp"),
        ),
        check_vma=False,
    )
```

```python
import functools

import jax
import jax.numpy as jnp
from jax import lax
from jax.experimental import pallas as pl
from jax.experimental.pallas import tpu as pltpu
from jax.sharding import PartitionSpec as P


CHUNKS = 2
ROWS = 256
COLUMNS = 256
ROOT = 0.7978845608028654
CUBIC = 0.044715
VMEM_LIMIT = 56 * 1024 * 1024


def swapped(array, axis, distance):
    return lax.ppermute(array, axis, [(i, i ^ 1 << distance) for i in range(lax.axis_size(axis))])


def dot(left, right):
    return jnp.dot(left, right, preferred_element_type=jnp.float32)


def dot_nt(left, right):
    return lax.dot_general(left, right, (((1,), (1,)), ((), ())), preferred_element_type=jnp.float32)


def dot_tn(left, right):
    return lax.dot_general(left, right, (((0,), (0,)), ((), ())), preferred_element_type=jnp.float32)


def sums_kernel(slabs, mu_ref, md_ref, *refs):
    x_ref, gy_ref = refs[:2]
    pairs = refs[2:1 + slabs]
    wu_ref, wd_ref, pre_ref, gh_ref = refs[1 + slabs:]
    width = x_ref.shape[1]
    left = [x_ref[...]]
    right = [gy_ref[...]]
    for k in range(slabs - 1):
        left.append(pairs[k][:, :width] * mu_ref[k].astype(jnp.bfloat16))
        right.append(pairs[k][:, width:] * md_ref[k].astype(jnp.bfloat16))
    hidden = wu_ref.shape[2]
    step = min(COLUMNS, hidden)
    @pl.loop(0, hidden // step)
    def _(block):
        cols = pl.ds(pl.multiple_of(block * step, step), step)
        total = dot(left[0], wu_ref[0, :, cols])
        for k in range(1, slabs):
            total += dot(left[k], wu_ref[k, :, cols])
        pre_ref[:, cols] = total
        total = dot_nt(right[0], wd_ref[0, cols, :])
        for k in range(1, slabs):
            total += dot_nt(right[k], wd_ref[k, cols, :])
        gh_ref[:, cols] = total


def smem():
    return pl.BlockSpec(memory_space=pltpu.SMEM)


def fixed(array):
    zeros = (0,) * array.ndim
    return pl.BlockSpec(array.shape, lambda i: zeros, pipeline_mode=pl.Buffered(1))


def by_rows(width):
    return pl.BlockSpec((ROWS, width), lambda i: (i, 0))


def sums(mu, md_partner, x, gy, pairs, w_up, w_down):
    slabs = len(pairs) + 1
    tokens, width = x.shape
    hidden = w_up.shape[2]
    flops = 4 * slabs * tokens * width * hidden
    return pl.pallas_call(
        functools.partial(sums_kernel, slabs),
        grid=(tokens // ROWS,),
        in_specs=[smem(), smem()] + [by_rows(width)] * 2 + [by_rows(2 * width)] * (slabs - 1) + [fixed(w_up), fixed(w_down)],
        out_specs=[by_rows(hidden)] * 2,
        out_shape=[jax.ShapeDtypeStruct((tokens, hidden), jnp.float32)] * 2,
        compiler_params=pltpu.CompilerParams(vmem_limit_bytes=VMEM_LIMIT),
        cost_estimate=pl.CostEstimate(flops=flops, bytes_accessed=8 * tokens * hidden + 4 * slabs * width * (tokens + hidden), transcendentals=0),
        name="sums",
    )(mu, md_partner, x, gy, *pairs, w_up, w_down)


def products_kernel(slabs, mu_ref, pre_ref, gh_ref, zs_ref, wu_ref, wd_ref, vu_ref, ud_ref, *outs):
    hid_ref, gp_ref, z_ref, out_ref, gx_ref = outs[:5]
    parts = outs[5:4 + slabs]
    width = wu_ref.shape[1]
    rank = vu_ref.shape[0]
    z_up = zs_ref[:, :rank]
    gz_down = zs_ref[:, rank:]
    hidden = wu_ref.shape[2]
    step = min(COLUMNS, hidden)
    for start in range(0, hidden, step):
        cols = slice(start, start + step)
        v = pre_ref[:, cols] + dot(z_up, vu_ref[:, cols])
        gh = gh_ref[:, cols] + dot_nt(gz_down, ud_ref[cols, :])
        square = v * v
        half_tanh = 0.5 * jnp.tanh(v * (ROOT + (ROOT * CUBIC) * square))
        gate = 0.5 + half_tanh
        hid_ref[:, cols] = (v * gate).astype(jnp.bfloat16)
        slope = gate + v * (0.5 - 2.0 * half_tanh * half_tanh) * (ROOT + (3.0 * ROOT * CUBIC) * square)
        gp_ref[:, cols] = (gh * slope).astype(jnp.bfloat16)
    hid = hid_ref[...]
    gp = gp_ref[...]
    for k in range(1, slabs):
        parts[k - 1][:, :width] = dot(hid, wd_ref[k]).astype(jnp.bfloat16)
        parts[k - 1][:, width:] = (dot_nt(gp, wu_ref[k]) * mu_ref[k - 1]).astype(jnp.bfloat16)
    out_ref[...] = dot(hid, wd_ref[0])
    gx_ref[...] = dot_nt(gp, wu_ref[0])
    z_ref[:, :rank] = dot(hid, ud_ref[...])
    z_ref[:, rank:] = dot_nt(gp, vu_ref[...])


def products(mu, pre, gh, zs, w_up, w_down, v_up, u_down):
    slabs, width, hidden = w_up.shape
    tokens = pre.shape[0]
    rank = v_up.shape[0]
    levels = slabs - 1
    shape = lambda n, dtype: jax.ShapeDtypeStruct((tokens, n), dtype)
    flops = 4 * tokens * hidden * (slabs * width + 2 * rank)
    got = pl.pallas_call(
        functools.partial(products_kernel, slabs),
        grid=(tokens // ROWS,),
        in_specs=[smem(), by_rows(hidden), by_rows(hidden), by_rows(2 * rank), fixed(w_up), fixed(w_down), fixed(v_up), fixed(u_down)],
        out_specs=[by_rows(hidden)] * 2 + [by_rows(2 * rank)] + [by_rows(width)] * 2 + [by_rows(2 * width)] * levels,
        out_shape=[shape(hidden, jnp.bfloat16)] * 2 + [shape(2 * rank, jnp.float32)] + [shape(width, jnp.float32)] * 2 + [shape(2 * width, jnp.bfloat16)] * levels,
        compiler_params=pltpu.CompilerParams(vmem_limit_bytes=VMEM_LIMIT),
        cost_estimate=pl.CostEstimate(flops=flops, bytes_accessed=12 * tokens * hidden + 4 * slabs * width * (tokens + hidden), transcendentals=tokens * hidden),
        name="products",
    )(mu, pre, gh, zs, w_up, w_down, v_up, u_down)
    return got[0], got[1], got[2], got[3], got[4], got[5:]


def low_rank_sum(partial):
    rounds = lax.axis_size("mp").bit_length() - 1
    index = lax.axis_index("mp")
    held = partial
    for level in range(rounds):
        bit = (index >> level) & 1
        half = held.shape[0] // 2
        sent = lax.dynamic_slice_in_dim(held, (1 - bit) * half, half)
        kept = lax.dynamic_slice_in_dim(held, bit * half, half)
        other = swapped(sent.astype(jnp.bfloat16) if level == 1 else sent, "mp", level)
        held = kept + other.astype(jnp.float32)
    held = held.astype(jnp.bfloat16)
    steps = {}
    for level in reversed(range(rounds)):
        bit = (index >> level) & 1
        other = swapped(held, "mp", level)
        steps[level] = other
        held = jnp.concatenate([jnp.where(bit == 0, held, other), jnp.where(bit == 0, other, held)])
    return held, steps


def summed_over_dp(array):
    if lax.axis_size("dp") == 1:
        return array
    return lax.psum(array.astype(jnp.bfloat16), "dp").astype(jnp.float32)


def sublayer(activations, w_up, w_down, u_up, v_up, u_down, v_down, mask_up, mask_down, grad_y):
    levels = mask_up.shape[0]
    slabs = levels + 1
    rank = v_up.shape[0]
    tokens = activations.shape[0]
    size = tokens // CHUNKS
    mu = mask_up[:, 0].astype(jnp.float32)
    md = mask_down[:, 0].astype(jnp.float32)
    zs, early = low_rank_sum(jnp.concatenate([dot(activations, u_up), dot_nt(grad_y, v_down)], axis=1))
    md_parts = []
    for k in range(levels):
        md_parts.append(swapped(md[k:k + 1], "mp", k))
    md_partner = jnp.concatenate(md_parts)
    width = activations.shape[1]
    pairs = []
    for c in range(CHUNKS):
        rows = slice(c * size, (c + 1) * size)
        both = jnp.concatenate([activations[rows], grad_y[rows]], axis=1)
        received = []
        for k in range(levels):
            sent = both if c == 0 else lax.optimization_barrier((both, early[k]))[0]
            received.append(swapped(sent, "mp", k))
        pairs.append(received)
    x_chunks = [[activations[c * size:(c + 1) * size]] + [p[:, :width] for p in pairs[c]] for c in range(CHUNKS)]
    gy_chunks = [[grad_y[c * size:(c + 1) * size]] + [p[:, width:] for p in pairs[c]] for c in range(CHUNKS)]
    stages, arrived = [], []
    for c in range(CHUNKS):
        pre, gh = sums(mu, md_partner, x_chunks[c][0], gy_chunks[c][0], pairs[c], w_up, w_down)
        stages.append(products(mu, pre, gh, zs[c * size:(c + 1) * size], w_up, w_down, v_up, u_down))
        received = []
        for k in range(levels):
            received.append(swapped(stages[c][5][k], "mp", k))
        arrived.append(received)
    z_late = low_rank_sum(jnp.concatenate([stage[2] for stage in stages]))[0]
    outputs, grad_xs = [], []
    for c in range(CHUNKS):
        rows = slice(c * size, (c + 1) * size)
        out = stages[c][3] + dot(z_late[rows, :rank], v_down)
        gx = stages[c][4] + dot_nt(z_late[rows, rank:], u_up)
        for k in range(levels):
            out = out + md[k] * arrived[c][k][:, :width].astype(jnp.float32)
            gx = gx + arrived[c][k][:, width:].astype(jnp.float32)
        outputs.append(out.astype(jnp.bfloat16))
        grad_xs.append(gx.astype(jnp.bfloat16))
    grad_w_down, grad_w_up = [], []
    for k in range(slabs):
        down = sum(dot_tn(stages[c][0], gy_chunks[c][k]) for c in range(CHUNKS))
        up = sum(dot_tn(x_chunks[c][k], stages[c][1]) for c in range(CHUNKS))
        grad_w_down.append(down if k == 0 else down * md_partner[k - 1])
        grad_w_up.append(up if k == 0 else up * mu[k - 1])
    grads = (
        jnp.stack(grad_w_up),
        jnp.stack(grad_w_down),
        dot_tn(activations, z_late[:, rank:]),
        sum(dot_tn(zs[c * size:(c + 1) * size, :rank], stages[c][1]) for c in range(CHUNKS)),
        sum(dot_tn(stages[c][0], zs[c * size:(c + 1) * size, rank:]) for c in range(CHUNKS)),
        dot_tn(z_late[:, :rank], grad_y),
    )
    grads = tuple(summed_over_dp(g) for g in grads)
    return (jnp.concatenate(outputs), jnp.concatenate(grad_xs)) + grads


def solution(mesh):
    placed = (
        P("dp", "mp"),
        P(None, None, "mp"),
        P(None, "mp", None),
        P("mp", None),
        P(None, "mp"),
        P("mp", None),
        P(None, "mp"),
        P(None, "mp"),
        P(None, "mp"),
        P("dp", "mp"),
    )
    return jax.shard_map(
        sublayer,
        mesh=mesh,
        in_specs=placed,
        out_specs=(
            P("dp", "mp"),
            P("dp", "mp"),
            P(None, None, "mp"),
            P(None, "mp", None),
            P("mp", None),
            P(None, "mp"),
            P("mp", None),
            P(None, "mp"),
        ),
        check_vma=False,
    )
```
